32 devices in a mesh: row: 8 (over z, core), col: 4 (over y, x).
Axes of the slice: x: 2, y: 2, z: 4, core: 2. Of those that a mesh axis runs over, the one named last changes fastest.
Arguments:
- points: bfloat16 [2048, 1024], P(('row', 'col')), may hold values from -6 to 6
- factor: float32 [2048, 256], P(('row', 'col')), may hold values from 0 to 1
Outputs:
- factor_out: float32 [2048, 256], P(('row', 'col'))
The draws below stay inside these ranges and needn't reach their ends.
All inputs are finite; a program needn't handle non-finite values.
Results may differ from the reference program's by a relative error of at most 0.002.
The reference program's roundings to bfloat16 on the way count: a program that leaves them out, or rounds other values in their place, can miss the bound.
Values may be sent and summed in bfloat16 or wider, within the bound.
A program may use at most 64 MiB of HBM per device.

```python
import math
import jax
import jax.numpy as jnp
from jax import lax

EMBED_WIDTH = 1024
R = 256
ITERS = 2
NPTS = 2048


def level_of(key, shape, split, least, top_value):
    factor_of, own = 1.0, jax.random.fold_in(key, 6)
    for axis_at, blocks in split:
        steps = jnp.exp(jax.random.uniform(jax.random.fold_in(own, axis_at), (blocks,), jnp.float32, least / len(split), top_value / len(split)))
        factor_of = factor_of * jnp.repeat(steps, shape[axis_at] // blocks).reshape([-1 if axis == axis_at else 1 for axis in range(len(shape))])
    return factor_of


def gaussian(rng, dims, spread, reach, shards=(), kind=jnp.bfloat16):
    entries = jax.random.normal(rng, dims, jnp.float32) * spread
    if len(shards) > 0:
        entries = level_of(rng, dims, shards, -0.22, 0.18) * entries
    return jnp.clip(entries, min=-reach, max=reach).astype(kind)


def setup_inputs(seed: int = 0) -> dict:
    arg_keys = jax.random.split(jax.random.key(seed), 3)
    points = gaussian(arg_keys[0], (NPTS, EMBED_WIDTH), 1.0, 6.0, ((0, 32),))
    factor = jnp.clip(1.0 * jax.random.uniform(arg_keys[1], (NPTS, R), jnp.float32) ** level_of(arg_keys[1], (NPTS, R), ((0, 32),), -0.2, 0.2), 0.0, 1.0)
    return dict(points=points, factor=factor)


def reference(points, factor):
    data = points.astype(jnp.float32)
    total = data.shape[0]
    rank = factor.shape[1]
    block_slab = math.gcd(512, total)
    nblocks = total // block_slab
    squared_norms = lax.optimization_barrier(jnp.sum(data * data, axis=1))

    def kernel_row_slab(index):
        offset_begin = (index * block_slab).astype(jnp.int32)
        rows = lax.dynamic_slice_in_dim(data, offset_begin, block_slab, 0)
        row_squared_norm = lax.dynamic_slice_in_dim(squared_norms, offset_begin, block_slab, 0)
        gram_matrix = jnp.dot(rows, data.T, precision=lax.Precision.HIGHEST)
        return jnp.exp((2.0 * gram_matrix - row_squared_norm[:, None] - squared_norms[None, :]) * (0.5 / EMBED_WIDTH))
    indices = jnp.arange(nblocks, dtype=jnp.int32)
    rowsum = lax.map(lambda i: lax.optimization_barrier(jnp.sum(kernel_row_slab(i), axis=1)), indices).reshape(total)
    grand = jnp.sum(rowsum)
    means = rowsum / total

    def affinity_rows(index):
        offset_begin = (index * block_slab).astype(jnp.int32)
        kern = kernel_row_slab(index)
        mine = lax.dynamic_slice_in_dim(means, offset_begin, block_slab, 0)
        return (kern - mine[:, None] - means[None, :] + grand / (total * total)).astype(jnp.bfloat16)
    unit = 2.0 / math.sqrt(total * rank)
    h = factor * unit
    for step in range(ITERS):
        hb = lax.optimization_barrier(h.astype(jnp.bfloat16)).astype(jnp.float32)
        ah = lax.map(lambda i: jnp.dot(affinity_rows(i).astype(jnp.float32), hb, precision=lax.Precision.HIGHEST), indices).reshape(total, rank)
        hh = jnp.dot(h.T, h, precision=lax.Precision.HIGHEST)
        scale = 0.5 / jnp.sqrt(jnp.sum(hh * hh) + 1e-06)
        h = jnp.maximum(h - scale * (jnp.dot(h, hh, precision=lax.Precision.HIGHEST) - ah), 0.0)
    return h / unit
```

```python
import functools
import math

import jax
import jax.numpy as jnp
from jax import lax
from jax.experimental import pallas as pl
from jax.experimental.pallas import tpu as pltpu
from jax.sharding import PartitionSpec as P

MESH = pl.DeviceIdType.MESH


def kernel(nrow, ncol, side, pts_ref, fac_ref, out_ref, buf, hbuf, kern, aff, mg, ssem, rsem, hssem, hrsem, mssem, mrsem):
    nz, plane = nrow // 2, ncol
    nchips = nz * plane
    rows, width = pts_ref.shape
    rank = fac_ref.shape[1]
    total = rows * nrow * ncol
    unit = 2.0 / math.sqrt(total * rank)
    row, col = lax.axis_index("row"), lax.axis_index("col")
    z, core = row // 2, row % 2
    y, x = col // side, col % side
    own = z * plane + col

    def chip_of(kz, ka, kb, sign):
        ky = ka * (1 - core) + kb * core
        kx = ka * core + kb * (1 - core)
        zz = (z + sign * kz + nz) % nz
        yy = (y + sign * ky + side) % side
        xx = (x + sign * kx + side) % side
        return zz, yy * side + xx

    def number(kz, ka, kb):
        return (kz * side + ka) * side + kb

    def slot_of(kz, ka, kb):
        zz, cc = chip_of(kz, ka, kb, -1)
        return zz * plane + cc

    barrier = pltpu.get_barrier_semaphore()
    peers = [(kz, 0, 0) for kz in range(1, nz)] + [(0, k, 0) for k in range(1, side)] + [(0, 0, k) for k in range(1, side)]
    for peer in peers:
        zz, cc = chip_of(*peer, 1)
        pl.semaphore_signal(barrier, inc=1, device_id=(zz * 2 + core, cc), device_id_type=MESH)
    pl.semaphore_signal(barrier, inc=1, device_id=(z * 2 + 1 - core, col), device_id_type=MESH)

    h = fac_ref[...] * unit
    buf[own, core, :, :width] = pts_ref[...]
    buf[own, core, :, width:] = h.astype(jnp.bfloat16)
    pl.semaphore_wait(barrier, len(peers) + 1)

    def gather(ref, send_sem, recv_sem, ready):
        started = []

        def copy(source, number_there, device):
            block = ref.at[source, core]
            return pltpu.make_async_remote_copy(
                src_ref=block,
                dst_ref=block,
                send_sem=send_sem.at[number_there],
                recv_sem=recv_sem.at[number_there],
                device_id=device,
                device_id_type=MESH,
            )

        def send(source, number_there, device):
            op = copy(source, number_there, device)
            op.start()
            started.append(op)

        def arrive(slot, core_there, number_here):
            block = ref.at[slot, core_there]
            pltpu.make_async_remote_copy(
                src_ref=block,
                dst_ref=block,
                send_sem=send_sem.at[number_here],
                recv_sem=recv_sem.at[number_here],
                device_id=(z * 2 + 1 - core, col),
                device_id_type=MESH,
            ).wait_recv()

        def handle(kz, ka, kb):
            source = slot_of(kz, ka, kb)
            if kz or ka or kb:
                arrive(source, core, number(kz, ka, kb))
            if not (kz or ka or kb):
                for k in range(1, nz):
                    zz, cc = chip_of(k, 0, 0, 1)
                    send(source, number(k, 0, 0), (zz * 2 + core, cc))
            if not kb:
                if not ka:
                    for k in range(1, side):
                        zz, cc = chip_of(0, k, 0, 1)
                        send(source, number(kz, k, 0), (zz * 2 + core, cc))
                for k in range(1, side):
                    zz, cc = chip_of(0, 0, k, 1)
                    send(source, number(kz, ka, k), (zz * 2 + core, cc))
            send(source, nchips + number(kz, ka, kb), (z * 2 + 1 - core, col))

        for t in range(nz + 3):
            if t < nz:
                handle(t, 0, 0)
            if 0 <= t - 1 < nz:
                for ka in range(1, side):
                    handle(t - 1, ka, 0)
            if 0 <= t - 2 < nz:
                for ka in range(side):
                    for kb in range(1, side):
                        handle(t - 2, ka, kb)
            if 0 <= t - 3 < nz:
                for ka in range(side):
                    for kb in range(side):
                        arrive(slot_of(t - 3, kb, ka), 1 - core, nchips + number(t - 3, ka, kb))
                ready((z - (t - 3) + nz) % nz)
        return started

    points = pts_ref[...]
    own32 = points.astype(jnp.float32)
    own_sq = jnp.sum(own32 * own32, axis=1, keepdims=True)
    pair = 2 if plane % 2 == 0 else 1
    wide = pair * 2 * rows

    sums = []

    def make_kernel(zz):
        def body(i, acc):
            block = buf[pl.ds(zz * plane + i * pair, pair), :, :, :width].reshape(wide, width)
            gram = lax.dot_general(points, block, (((1,), (1,)), ((), ())), preferred_element_type=jnp.float32)
            sq = None
            for k in range(0, width, 128):
                piece = block[:, k : k + 128].astype(jnp.float32)
                sq = piece * piece if sq is None else sq + piece * piece
            sq = jnp.sum(sq.T, axis=0, keepdims=True)
            kb = jnp.exp((2.0 * gram - own_sq - sq) * (0.5 / width))
            kern[zz, :, pl.ds(pl.multiple_of(i * wide, wide), wide)] = kb
            return acc + jnp.sum(kb, axis=1, keepdims=True)

        sums.append(lax.fori_loop(0, plane // pair, body, jnp.zeros((rows, 1), jnp.float32)))

    sends = gather(buf, ssem, rsem, make_kernel)
    row_sum = functools.reduce(jnp.add, sums)

    lanes = lax.broadcasted_iota(jnp.int32, (rows, 2 * rows), 1)
    subl = lax.broadcasted_iota(jnp.int32, (rows, 2 * rows), 0)
    spread = jnp.sum(jnp.where(lanes == subl + core * rows, row_sum, 0.0), axis=0, keepdims=True)
    mine = own * 2 + core
    mg[mine] = spread

    def row_sums(kr, kc, sign):
        rr, cc = (row + sign * kr + nrow) % nrow, (col + sign * kc + ncol) % ncol
        k = kr * ncol + kc
        slot = mine if sign > 0 else ((rr // 2) * plane + cc) * 2 + rr % 2
        return pltpu.make_async_remote_copy(
            src_ref=mg.at[slot],
            dst_ref=mg.at[slot],
            send_sem=mssem.at[k],
            recv_sem=mrsem.at[k],
            device_id=(rr, cc),
            device_id_type=MESH,
        )

    def each(action):
        def body(k, carry):
            action(k // ncol, k % ncol)
            return carry

        lax.fori_loop(1, nrow * ncol, body, 0)

    each(lambda kr, kc: row_sums(kr, kc, 1).start())

    def gram_of(load):
        hh = None
        for zz in range(nz):
            hz = load(zz)
            part = lax.dot_general(hz, hz, (((0,), (0,)), ((), ())), preferred_element_type=jnp.float32)
            hh = part if hh is None else hh + part
        return hh

    def load_first(zz):
        return buf[zz * plane : (zz + 1) * plane, :, :, width:].reshape(plane * 2 * rows, rank)

    def load_later(zz):
        return hbuf[zz * plane : (zz + 1) * plane].reshape(plane * 2 * rows, rank)

    def pull(h, hh):
        scale = 0.5 / jnp.sqrt(jnp.sum(hh * hh, keepdims=True) + 1e-06)
        return scale, jnp.dot(h, hh, precision=lax.Precision.HIGHEST, preferred_element_type=jnp.float32)

    scale, hhh = pull(h, gram_of(load_first))
    for op in sends:
        op.wait_send()
    each(lambda kr, kc: row_sums(kr, kc, -1).wait_recv())
    each(lambda kr, kc: row_sums(kr, kc, 1).wait_send())

    grand = jnp.sum(jnp.sum(mg[...], axis=0), axis=1, keepdims=True) / (total * total)
    row_mean = row_sum / total
    shift = grand - row_mean
    ah = jnp.zeros((rows, rank), jnp.float32)
    for zz in range(nz):
        for i in range(plane):
            c = zz * plane + i
            col_mean = (mg[2 * c] + mg[2 * c + 1]) / total
            span = slice(i * 2 * rows, (i + 1) * 2 * rows)
            aff[zz, :, span] = (kern[zz, :, span] - row_mean - col_mean + grand).astype(jnp.bfloat16)
        ah += jnp.dot(aff[zz], load_first(zz), preferred_element_type=jnp.float32)
    h = jnp.maximum(h - scale * (hhh - ah), 0.0)

    hbuf[own, core] = h.astype(jnp.bfloat16)
    partial = []

    def step_two(zz):
        hz = hbuf[pl.ds(zz * plane, plane)].reshape(plane * 2 * rows, rank)
        partial.append(
            (
                jnp.dot(aff[zz], hz, preferred_element_type=jnp.float32),
                lax.dot_general(hz, hz, (((0,), (0,)), ((), ())), preferred_element_type=jnp.float32),
            )
        )

    sends = gather(hbuf, hssem, hrsem, step_two)
    ah = functools.reduce(jnp.add, [p[0] for p in partial])
    scale, hhh = pull(h, functools.reduce(jnp.add, [p[1] for p in partial]))
    out_ref[...] = jnp.maximum(h - scale * (hhh - ah), 0.0) / unit
    for op in sends:
        op.wait_send()


def solution(mesh):
    nrow, ncol = mesh.shape["row"], mesh.shape["col"]
    side = math.isqrt(ncol)
    nz = nrow // 2
    nchips = nz * ncol

    def shards(points, factor):
        rows, width = points.shape
        rank = factor.shape[1]
        return pl.pallas_call(
            functools.partial(kernel, nrow, ncol, side),
            out_shape=jax.ShapeDtypeStruct((rows, rank), jnp.float32),
            in_specs=[pl.BlockSpec(memory_space=pltpu.VMEM)] * 2,
            out_specs=pl.BlockSpec(memory_space=pltpu.VMEM),
            scratch_shapes=[
                pltpu.VMEM((nchips, 2, rows, width + rank), jnp.bfloat16),
                pltpu.VMEM((nchips, 2, rows, rank), jnp.bfloat16),
                pltpu.VMEM((nz, rows, ncol * 2 * rows), jnp.float32),
                pltpu.VMEM((nz, rows, ncol * 2 * rows), jnp.bfloat16),
                pltpu.VMEM((nchips * 2, 1, 2 * rows), jnp.float32),
                pltpu.SemaphoreType.DMA((2 * nchips,)),
                pltpu.SemaphoreType.DMA((2 * nchips,)),
                pltpu.SemaphoreType.DMA((2 * nchips,)),
                pltpu.SemaphoreType.DMA((2 * nchips,)),
                pltpu.SemaphoreType.DMA((nrow * ncol,)),
                pltpu.SemaphoreType.DMA((nrow * ncol,)),
            ],
            compiler_params=pltpu.CompilerParams(
                collective_id=0, has_side_effects=True, vmem_limit_bytes=67043328
            ),
        )(points, factor)

    spec = P(("row", "col"), None)
    return jax.shard_map(shards, mesh=mesh, in_specs=(spec, spec), out_specs=spec, check_vma=False)
```

```python
import functools
import math

import jax
import jax.numpy as jnp
from jax import lax
from jax.experimental import pallas as pl
from jax.experimental.pallas import tpu as pltpu
from jax.sharding import PartitionSpec as P

MESH = pl.DeviceIdType.MESH
EARLY = 3


def kernel(nrow, ncol, side, pts_ref, fac_ref, out_ref, rbuf, cbuf, first, later, kern, asend, arecv, rsum, csum, tsum, sems):
    nz, plane = nrow // 2, ncol
    rows, width = pts_ref.shape
    rank = fac_ref.shape[1]
    total = rows * nrow * ncol
    unit = 2.0 / math.sqrt(total * rank)
    row, col = lax.axis_index("row"), lax.axis_index("col")
    z, core = row // 2, row % 2
    y, x = col // side, col % side
    partner = (z * 2 + 1 - core, col)

    def at(kz, ka, kb, sign):
        ky = ka * (1 - core) + kb * core
        kx = ka * core + kb * (1 - core)
        zz = (z + sign * kz + nz) % nz
        yy = (y + sign * ky + side) % side
        xx = (x + sign * kx + side) % side
        return zz, yy * side + xx

    def number(kz, ka, kb):
        return (kz * side + ka) * side + kb

    def remote(src, dst, pair, index, device):
        return pltpu.make_async_remote_copy(
            src_ref=src,
            dst_ref=dst,
            send_sem=pair[0].at[index],
            recv_sem=pair[1].at[index],
            device_id=device,
            device_id_type=MESH,
        )

    started = []

    def send(block, pair, index, device):
        op = remote(block, block, pair, index, device)
        op.start()
        started.append(op)

    def arrive(block, pair, index):
        remote(block, block, pair, index, partner).wait_recv()

    barrier = pltpu.get_barrier_semaphore()
    steps = range(1, side)
    peers = [(kz, 0, 0) for kz in range(1, nz)] + [(0, k, 0) for k in steps] + [(0, 0, k) for k in steps]
    for peer in peers:
        zz, cc = at(*peer, 1)
        pl.semaphore_signal(barrier, inc=1, device_id=(zz * 2 + core, cc), device_id_type=MESH)
    pl.semaphore_signal(barrier, inc=1, device_id=partner, device_id_type=MESH)

    h = fac_ref[...] * unit
    rbuf[col] = pts_ref[...]
    cbuf[z, core] = pts_ref[...]
    first[col, z, core] = h.astype(jnp.bfloat16)
    pl.semaphore_wait(barrier, len(peers) + 1)

    def gather(ref, pair):
        nchips = nz * plane

        def handle(kz, ka, kb):
            zz, cc = at(kz, ka, kb, -1)
            block = ref.at[cc, zz, core]
            if kz or ka or kb:
                arrive(block, pair, number(kz, ka, kb))
            else:
                for k in range(1, nz):
                    there, _ = at(k, 0, 0, 1)
                    send(block, pair, number(k, 0, 0), (there * 2 + core, col))
            if not kb:
                if not ka:
                    for k in steps:
                        _, there = at(0, k, 0, 1)
                        send(block, pair, number(kz, k, 0), (row, there))
                for k in steps:
                    _, there = at(0, 0, k, 1)
                    send(block, pair, number(kz, ka, k), (row, there))
            send(block, pair, nchips + number(kz, ka, kb), partner)

        def stage(t):
            if t < nz:
                handle(t, 0, 0)
            if 0 <= t - 1 < nz:
                for ka in steps:
                    handle(t - 1, ka, 0)
            if 0 <= t - 2 < nz:
                for ka in range(side):
                    for kb in steps:
                        handle(t - 2, ka, kb)
            if 0 <= t - 3 < nz:
                for ka in range(side):
                    for kb in range(side):
                        zz, cc = at(t - 3, kb, ka, -1)
                        arrive(ref.at[cc, zz, 1 - core], pair, nchips + number(t - 3, ka, kb))
                return (z - (t - 3) + nz) % nz
            return None

        return stage

    zpair, ppair = sems[0], sems[1]
    for k in range(1, nz):
        there, _ = at(k, 0, 0, 1)
        send(cbuf.at[z, core], zpair, k, (there * 2 + core, col))
    for k in steps:
        _, there = at(0, k, 0, 1)
        send(rbuf.at[col], ppair, number(0, k, 0), (row, there))
    for k in steps:
        _, there = at(0, 0, k, 1)
        send(rbuf.at[col], ppair, number(0, 0, k), (row, there))
    send(cbuf.at[z, core], zpair, nz, partner)
    for ka in steps:
        _, cc = at(0, ka, 0, -1)
        arrive(rbuf.at[cc], ppair, number(0, ka, 0))
        for k in steps:
            _, there = at(0, 0, k, 1)
            send(rbuf.at[cc], ppair, number(0, ka, k), (row, there))
    for ka in range(side):
        for kb in steps:
            _, cc = at(0, ka, kb, -1)
            arrive(rbuf.at[cc], ppair, number(0, ka, kb))

    def squares(block):
        acc = None
        for k in range(0, width, 128):
            piece = block[:, k : k + 128].astype(jnp.float32)
            acc = piece * piece if acc is None else acc + piece * piece
        return acc

    band, wide = plane * rows, 2 * rows
    tall = min(band, 256)
    row_acc = [None] * (band // tall)
    row_sq = []
    for r in range(band // tall):
        group = tall // rows
        row_sq.append(jnp.sum(squares(rbuf[r * group : (r + 1) * group].reshape(tall, width)), axis=1, keepdims=True))
    mine = row
    tot = jnp.zeros((1, wide), jnp.float32)
    for kz in range(nz):
        zz = (z - kz + nz) % nz
        if kz:
            arrive(cbuf.at[zz, core], zpair, kz)
            send(cbuf.at[zz, core], zpair, nz + kz, partner)
        arrive(cbuf.at[zz, 1 - core], zpair, nz + kz)
        block = cbuf[zz].reshape(wide, width)
        col_sq = jnp.sum(squares(block).T, axis=0, keepdims=True)
        col_acc = jnp.zeros((1, wide), jnp.float32)
        for r in range(band // tall):
            group = tall // rows
            mat = rbuf[r * group : (r + 1) * group].reshape(tall, width)
            gram = lax.dot_general(mat, block, (((1,), (1,)), ((), ())), preferred_element_type=jnp.float32)
            k = jnp.exp((2.0 * gram - row_sq[r] - col_sq) * (0.5 / width))
            kern[zz, r * tall : (r + 1) * tall, :] = k
            row_acc[r] = k if row_acc[r] is None else row_acc[r] + k
            col_acc += jnp.sum(k, axis=0, keepdims=True)
        csum[mine, pl.ds(zz, 1), :] = col_acc
        tot += col_acc
    for r in range(band // tall):
        rsum[col, :, r * tall : (r + 1) * tall] = jnp.sum(row_acc[r].T, axis=0, keepdims=True)
    mydev = row * ncol + col
    tsum[mydev] = tot

    rpair, cpair, tpair = sems[2], sems[3], sems[4]

    def row_copy(k, sign):
        cc = (col + sign * k + ncol) % ncol
        block = rsum.at[col if sign > 0 else cc]
        return remote(block, block, rpair, k, (row, cc))

    def col_copy(k, sign):
        rr = (row + sign * k + nrow) % nrow
        block = csum.at[row if sign > 0 else rr]
        return remote(block, block, cpair, k, (rr, col))

    def tot_copy(k, sign):
        rr, cc = (row + sign * (k // ncol) + nrow) % nrow, (col + sign * (k % ncol) + ncol) % ncol
        block = tsum.at[mydev if sign > 0 else rr * ncol + cc]
        return remote(block, block, tpair, k, (rr, cc))

    def aff_copy(k, sign):
        cc = (col + sign * k + ncol) % ncol
        return remote(asend.at[cc], arecv.at[col if sign > 0 else cc], sems[5], k, (row, cc))

    def each(count, action):
        def body(k, carry):
            action(k)
            return carry

        lax.fori_loop(1, count, body, 0)

    each(ncol, lambda k: row_copy(k, 1).start())
    each(nrow, lambda k: col_copy(k, 1).start())
    each(nrow * ncol, lambda k: tot_copy(k, 1).start())

    def gram_of(block):
        return lax.dot_general(block, block, (((0,), (0,)), ((), ())), preferred_element_type=jnp.float32)

    def pull(h, hh):
        scale = 0.5 / jnp.sqrt(jnp.sum(hh * hh, keepdims=True) + 1e-06)
        return scale, jnp.dot(h, hh, precision=lax.Precision.HIGHEST, preferred_element_type=jnp.float32)

    stage = gather(first, sems[6])
    for t in range(EARLY):
        stage(t)

    each(ncol, lambda k: row_copy(k, -1).wait_recv())
    each(nrow, lambda k: col_copy(k, -1).wait_recv())
    each(nrow * ncol, lambda k: tot_copy(k, -1).wait_recv())
    grand = jnp.sum(jnp.sum(tsum[...], axis=0), axis=1, keepdims=True) / (total * total)
    col_mean = jnp.sum(csum[...], axis=0) / total
    row_mean = jnp.sum(rsum[...], axis=0) / total
    for r in range(band // tall):
        group = tall // rows
        mean_r = jnp.broadcast_to(row_mean[:, r * tall : (r + 1) * tall], (wide, tall)).T
        for zz in range(nz):
            k = kern[zz, r * tall : (r + 1) * tall, :] - mean_r - col_mean[zz : zz + 1, :] + grand
            asend[r * group : (r + 1) * group, zz] = k.astype(jnp.bfloat16).reshape(group, rows, wide)
    arecv[col] = asend[col]
    each(ncol, lambda k: aff_copy(k, 1).start())

    hh = jnp.zeros((rank, rank), jnp.float32)
    for t in range(EARLY, nz + 3):
        stage(t)
    for zz in range(nz):
        hh += gram_of(first[:, zz].reshape(plane * wide, rank))
    scale, hhh = pull(h, hh)
    each(ncol, lambda k: aff_copy(k, -1).wait_recv())

    def panel(zz):
        return jnp.concatenate([arecv[c, zz] for c in range(plane)], axis=1)

    ah = jnp.zeros((rows, rank), jnp.float32)
    for zz in range(nz):
        ah += jnp.dot(panel(zz), first[:, zz].reshape(plane * wide, rank), preferred_element_type=jnp.float32)
    h = jnp.maximum(h - scale * (hhh - ah), 0.0)

    later[col, z, core] = h.astype(jnp.bfloat16)
    stage = gather(later, sems[7])
    ah = jnp.zeros((rows, rank), jnp.float32)
    hh = jnp.zeros((rank, rank), jnp.float32)
    for t in range(nz + 3):
        zz = stage(t)
        if zz is not None:
            block = later[:, zz].reshape(plane * wide, rank)
            ah += jnp.dot(panel(zz), block, preferred_element_type=jnp.float32)
            hh += gram_of(block)
    scale, hhh = pull(h, hh)
    out_ref[...] = jnp.maximum(h - scale * (hhh - ah), 0.0) / unit
    for op in started:
        op.wait_send()
    each(ncol, lambda k: row_copy(k, 1).wait_send())
    each(nrow, lambda k: col_copy(k, 1).wait_send())
    each(nrow * ncol, lambda k: tot_copy(k, 1).wait_send())
    each(ncol, lambda k: aff_copy(k, 1).wait_send())


def solution(mesh):
    nrow, ncol = mesh.shape["row"], mesh.shape["col"]
    side = math.isqrt(ncol)
    nz = nrow // 2
    nchips = nz * ncol

    def shards(points, factor):
        rows, width = points.shape
        rank = factor.shape[1]
        wide = 2 * rows
        counts = (2 * nz, ncol, ncol, nrow, nrow * ncol, ncol, 2 * nchips, 2 * nchips)
        return pl.pallas_call(
            functools.partial(kernel, nrow, ncol, side),
            out_shape=jax.ShapeDtypeStruct((rows, rank), jnp.float32),
            in_specs=[pl.BlockSpec(memory_space=pltpu.VMEM)] * 2,
            out_specs=pl.BlockSpec(memory_space=pltpu.VMEM),
            scratch_shapes=[
                pltpu.VMEM((ncol, rows, width), jnp.bfloat16),
                pltpu.VMEM((nz, 2, rows, width), jnp.bfloat16),
                pltpu.VMEM((ncol, nz, 2, rows, rank), jnp.bfloat16),
                pltpu.VMEM((ncol, nz, 2, rows, rank), jnp.bfloat16),
                pltpu.VMEM((nz, ncol * rows, wide), jnp.float32),
                pltpu.VMEM((ncol, nz, rows, wide), jnp.bfloat16),
                pltpu.VMEM((ncol, nz, rows, wide), jnp.bfloat16),
                pltpu.VMEM((ncol, 1, ncol * rows), jnp.float32),
                pltpu.VMEM((nrow, nz, wide), jnp.float32),
                pltpu.VMEM((nrow * ncol, 1, wide), jnp.float32),
                [(pltpu.SemaphoreType.DMA((n,)), pltpu.SemaphoreType.DMA((n,))) for n in counts],
            ],
            compiler_params=pltpu.CompilerParams(
                collective_id=0, has_side_effects=True, vmem_limit_bytes=67043328
            ),
        )(points, factor)

    spec = P(("row", "col"), None)
    return jax.shard_map(shards, mesh=mesh, in_specs=(spec, spec), out_specs=spec, check_vma=False)
```

```python
import functools
import math

import jax
import jax.numpy as jnp
from jax import lax
from jax.experimental import pallas as pl
from jax.experimental.pallas import tpu as pltpu
from jax.sharding import PartitionSpec as P

MESH = pl.DeviceIdType.MESH
EARLY = 3


def kernel(nrow, ncol, side, pts_ref, fac_ref, out_ref, rbuf, cbuf, first, later, kern, asend, arecv, rsum, csum, tsum, sems):
    nz, plane = nrow // 2, ncol
    rows, width = pts_ref.shape
    rank = fac_ref.shape[1]
    total = rows * nrow * ncol
    unit = 2.0 / math.sqrt(total * rank)
    row, col = lax.axis_index("row"), lax.axis_index("col")
    z, core = row // 2, row % 2
    y, x = col // side, col % side
    partner = (z * 2 + 1 - core, col)

    def across(kz, sign):
        if nz & (nz - 1):
            return (z + sign * kz + nz) % nz
        zz, bit = z, 1
        while bit < nz:
            if kz & bit:
                zz = zz + bit - 2 * bit * ((z // bit) % 2)
            bit *= 2
        return zz

    def at(kz, ka, kb, sign):
        ky = ka * (1 - core) + kb * core
        kx = ka * core + kb * (1 - core)
        zz = across(kz, sign)
        yy = (y + sign * ky + side) % side
        xx = (x + sign * kx + side) % side
        return zz, yy * side + xx

    def number(kz, ka, kb):
        return (kz * side + ka) * side + kb

    def remote(src, dst, pair, index, device):
        return pltpu.make_async_remote_copy(
            src_ref=src,
            dst_ref=dst,
            send_sem=pair[0].at[index],
            recv_sem=pair[1].at[index],
            device_id=device,
            device_id_type=MESH,
        )

    started = []

    def send(block, pair, index, device):
        op = remote(block, block, pair, index, device)
        op.start()
        started.append(op)

    def arrive(block, pair, index):
        remote(block, block, pair, index, partner).wait_recv()

    barrier = pltpu.get_barrier_semaphore()
    steps = range(1, side)
    peers = [(kz, 0, 0) for kz in range(1, nz)] + [(0, k, 0) for k in steps] + [(0, 0, k) for k in steps]
    for peer in peers:
        zz, cc = at(*peer, 1)
        pl.semaphore_signal(barrier, inc=1, device_id=(zz * 2 + core, cc), device_id_type=MESH)
    pl.semaphore_signal(barrier, inc=1, device_id=partner, device_id_type=MESH)

    h = fac_ref[...] * unit
    rbuf[col] = pts_ref[...]
    cbuf[z, core] = pts_ref[...]
    first[col, z, core] = h.astype(jnp.bfloat16)
    pl.semaphore_wait(barrier, len(peers) + 1)

    def gather(ref, pair):
        nchips = nz * plane

        def handle(kz, ka, kb):
            zz, cc = at(kz, ka, kb, -1)
            block = ref.at[cc, zz, core]
            if kz or ka or kb:
                arrive(block, pair, number(kz, ka, kb))
            else:
                for k in range(1, nz):
                    there, _ = at(k, 0, 0, 1)
                    send(block, pair, number(k, 0, 0), (there * 2 + core, col))
            if not kb:
                if not ka:
                    for k in steps:
                        _, there = at(0, k, 0, 1)
                        send(block, pair, number(kz, k, 0), (row, there))
                for k in steps:
                    _, there = at(0, 0, k, 1)
                    send(block, pair, number(kz, ka, k), (row, there))
            send(block, pair, nchips + number(kz, ka, kb), partner)

        def stage(t):
            if t < nz:
                handle(t, 0, 0)
            if 0 <= t - 1 < nz:
                for ka in steps:
                    handle(t - 1, ka, 0)
            if 0 <= t - 2 < nz:
                for ka in range(side):
                    for kb in steps:
                        handle(t - 2, ka, kb)
            if 0 <= t - 3 < nz:
                for ka in range(side):
                    for kb in range(side):
                        zz, cc = at(t - 3, kb, ka, -1)
                        arrive(ref.at[cc, zz, 1 - core], pair, nchips + number(t - 3, ka, kb))
                return across(t - 3, -1)
            return None

        return stage

    zpair, ppair = sems[0], sems[1]
    for k in range(1, nz):
        there, _ = at(k, 0, 0, 1)
        send(cbuf.at[z, core], zpair, k, (there * 2 + core, col))
    for k in steps:
        _, there = at(0, k, 0, 1)
        send(rbuf.at[col], ppair, number(0, k, 0), (row, there))
    for k in steps:
        _, there = at(0, 0, k, 1)
        send(rbuf.at[col], ppair, number(0, 0, k), (row, there))
    send(cbuf.at[z, core], zpair, nz, partner)
    stage = gather(first, sems[6])
    stage(0)
    for ka in steps:
        _, cc = at(0, ka, 0, -1)
        arrive(rbuf.at[cc], ppair, number(0, ka, 0))
        for k in steps:
            _, there = at(0, 0, k, 1)
            send(rbuf.at[cc], ppair, number(0, ka, k), (row, there))
    for ka in range(side):
        for kb in steps:
            _, cc = at(0, ka, kb, -1)
            arrive(rbuf.at[cc], ppair, number(0, ka, kb))

    def squares(block):
        acc = None
        for k in range(0, width, 128):
            piece = block[:, k : k + 128].astype(jnp.float32)
            acc = piece * piece if acc is None else acc + piece * piece
        return acc

    band, wide = plane * rows, 2 * rows
    tall = min(band, 256)
    row_acc = [None] * (band // tall)
    row_sq = []
    for r in range(band // tall):
        group = tall // rows
        row_sq.append(jnp.sum(squares(rbuf[r * group : (r + 1) * group].reshape(tall, width)), axis=1, keepdims=True))
    mine = row
    tot = jnp.zeros((1, wide), jnp.float32)
    for kz in range(nz):
        zz = across(kz, -1)
        if kz:
            arrive(cbuf.at[zz, core], zpair, kz)
            send(cbuf.at[zz, core], zpair, nz + kz, partner)
            stage(kz)
        arrive(cbuf.at[zz, 1 - core], zpair, nz + kz)
        block = cbuf[zz].reshape(wide, width)
        col_sq = jnp.sum(squares(block).T, axis=0, keepdims=True)
        col_acc = jnp.zeros((1, wide), jnp.float32)
        for r in range(band // tall):
            group = tall // rows
            mat = rbuf[r * group : (r + 1) * group].reshape(tall, width)
            gram = lax.dot_general(mat, block, (((1,), (1,)), ((), ())), preferred_element_type=jnp.float32)
            k = jnp.exp((2.0 * gram - row_sq[r] - col_sq) * (0.5 / width))
            kern[zz, r * tall : (r + 1) * tall, :] = k
            row_acc[r] = k if row_acc[r] is None else row_acc[r] + k
            col_acc += jnp.sum(k, axis=0, keepdims=True)
        csum[mine, pl.ds(zz, 1), :] = col_acc
        tot += col_acc
    for r in range(band // tall):
        rsum[col, :, r * tall : (r + 1) * tall] = jnp.sum(row_acc[r].T, axis=0, keepdims=True)
    mydev = row * ncol + col
    tsum[mydev] = tot

    rpair, cpair, tpair = sems[2], sems[3], sems[4]

    def row_copy(k, sign):
        cc = (col + sign * k + ncol) % ncol
        block = rsum.at[col if sign > 0 else cc]
        return remote(block, block, rpair, k, (row, cc))

    def col_copy(k, sign):
        rr = (row + sign * k + nrow) % nrow
        block = csum.at[row if sign > 0 else rr]
        return remote(block, block, cpair, k, (rr, col))

    def tot_copy(k, sign):
        rr, cc = (row + sign * (k // ncol) + nrow) % nrow, (col + sign * (k % ncol) + ncol) % ncol
        block = tsum.at[mydev if sign > 0 else rr * ncol + cc]
        return remote(block, block, tpair, k, (rr, cc))

    def aff_copy(k, sign):
        cc = (col + sign * k + ncol) % ncol
        return remote(asend.at[cc], arecv.at[col if sign > 0 else cc], sems[5], k, (row, cc))

    def each(count, action):
        def body(k, carry):
            action(k)
            return carry

        lax.fori_loop(1, count, body, 0)

    each(ncol, lambda k: row_copy(k, 1).start())
    each(nrow, lambda k: col_copy(k, 1).start())
    each(nrow * ncol, lambda k: tot_copy(k, 1).start())

    def gram_of(block):
        return lax.dot_general(block, block, (((0,), (0,)), ((), ())), preferred_element_type=jnp.float32)

    def pull(h, hh):
        scale = 0.5 / jnp.sqrt(jnp.sum(hh * hh, keepdims=True) + 1e-06)
        return scale, jnp.dot(h, hh, precision=lax.Precision.HIGHEST, preferred_element_type=jnp.float32)

    for t in range(nz, nz + EARLY):
        stage(t)

    each(ncol, lambda k: row_copy(k, -1).wait_recv())
    each(nrow, lambda k: col_copy(k, -1).wait_recv())
    each(nrow * ncol, lambda k: tot_copy(k, -1).wait_recv())
    grand = jnp.sum(jnp.sum(tsum[...], axis=0), axis=1, keepdims=True) / (total * total)
    col_mean = jnp.sum(csum[...], axis=0) / total
    row_mean = jnp.sum(rsum[...], axis=0) / total
    for r in range(band // tall):
        group = tall // rows
        mean_r = jnp.broadcast_to(row_mean[:, r * tall : (r + 1) * tall], (wide, tall)).T
        for zz in range(nz):
            k = kern[zz, r * tall : (r + 1) * tall, :] - mean_r - col_mean[zz : zz + 1, :] + grand
            asend[r * group : (r + 1) * group, zz] = k.astype(jnp.bfloat16).reshape(group, rows, wide)
    arecv[col] = asend[col]
    each(ncol, lambda k: aff_copy(k, 1).start())

    hh = jnp.zeros((rank, rank), jnp.float32)
    for t in range(nz + EARLY, nz + 3):
        stage(t)
    for zz in range(nz):
        hh += gram_of(first[:, zz].reshape(plane * wide, rank))
    scale, hhh = pull(h, hh)
    each(ncol, lambda k: aff_copy(k, -1).wait_recv())

    def panel(zz):
        return jnp.concatenate([arecv[c, zz] for c in range(plane)], axis=1)

    ah = jnp.zeros((rows, rank), jnp.float32)
    for zz in range(nz):
        ah += jnp.dot(panel(zz), first[:, zz].reshape(plane * wide, rank), preferred_element_type=jnp.float32)
    h = jnp.maximum(h - scale * (hhh - ah), 0.0)

    later[col, z, core] = h.astype(jnp.bfloat16)
    stage = gather(later, sems[7])
    ah = jnp.zeros((rows, rank), jnp.float32)
    hh = jnp.zeros((rank, rank), jnp.float32)
    for t in range(nz + 3):
        zz = stage(t)
        if zz is not None:
            block = later[:, zz].reshape(plane * wide, rank)
            ah += jnp.dot(panel(zz), block, preferred_element_type=jnp.float32)
            hh += gram_of(block)
    scale, hhh = pull(h, hh)
    out_ref[...] = jnp.maximum(h - scale * (hhh - ah), 0.0) / unit
    for op in started:
        op.wait_send()
    each(ncol, lambda k: row_copy(k, 1).wait_send())
    each(nrow, lambda k: col_copy(k, 1).wait_send())
    each(nrow * ncol, lambda k: tot_copy(k, 1).wait_send())
    each(ncol, lambda k: aff_copy(k, 1).wait_send())


def solution(mesh):
    nrow, ncol = mesh.shape["row"], mesh.shape["col"]
    side = math.isqrt(ncol)
    nz = nrow // 2
    nchips = nz * ncol

    def shards(points, factor):
        rows, width = points.shape
        rank = factor.shape[1]
        wide = 2 * rows
        counts = (2 * nz, ncol, ncol, nrow, nrow * ncol, ncol, 2 * nchips, 2 * nchips)
        return pl.pallas_call(
            functools.partial(kernel, nrow, ncol, side),
            out_shape=jax.ShapeDtypeStruct((rows, rank), jnp.float32),
            in_specs=[pl.BlockSpec(memory_space=pltpu.VMEM)] * 2,
            out_specs=pl.BlockSpec(memory_space=pltpu.VMEM),
            scratch_shapes=[
                pltpu.VMEM((ncol, rows, width), jnp.bfloat16),
                pltpu.VMEM((nz, 2, rows, width), jnp.bfloat16),
                pltpu.VMEM((ncol, nz, 2, rows, rank), jnp.bfloat16),
                pltpu.VMEM((ncol, nz, 2, rows, rank), jnp.bfloat16),
                pltpu.VMEM((nz, ncol * rows, wide), jnp.float32),
                pltpu.VMEM((ncol, nz, rows, wide), jnp.bfloat16),
                pltpu.VMEM((ncol, nz, rows, wide), jnp.bfloat16),
                pltpu.VMEM((ncol, 1, ncol * rows), jnp.float32),
                pltpu.VMEM((nrow, nz, wide), jnp.float32),
                pltpu.VMEM((nrow * ncol, 1, wide), jnp.float32),
                [(pltpu.SemaphoreType.DMA((n,)), pltpu.SemaphoreType.DMA((n,))) for n in counts],
            ],
            compiler_params=pltpu.CompilerParams(
                collective_id=0, has_side_effects=True, vmem_limit_bytes=67043328
            ),
        )(points, factor)

    spec = P(("row", "col"), None)
    return jax.shard_map(shards, mesh=mesh, in_specs=(spec, spec), out_specs=spec, check_vma=False)
```

```python
import functools
import math

import jax
import jax.numpy as jnp
from jax import lax
from jax.experimental import pallas as pl
from jax.experimental.pallas import tpu as pltpu
from jax.sharding import PartitionSpec as P

MESH = pl.DeviceIdType.MESH


def kernel(nrow, ncol, side, pts_ref, fac_ref, out_ref, rbuf, cbuf, first, later, kern, asend, arecv, rsum, csum, tsum, sems):
    nz, plane = nrow // 2, ncol
    rows, width = pts_ref.shape
    rank = fac_ref.shape[1]
    total = rows * nrow * ncol
    unit = 2.0 / math.sqrt(total * rank)
    row, col = lax.axis_index("row"), lax.axis_index("col")
    z, core = row // 2, row % 2
    y, x = col // side, col % side
    partner = (z * 2 + 1 - core, col)

    def across(kz, sign):
        if nz & (nz - 1):
            return (z + sign * kz + nz) % nz
        zz, bit = z, 1
        while bit < nz:
            if kz & bit:
                zz = zz + bit - 2 * bit * ((z // bit) % 2)
            bit *= 2
        return zz

    def at(kz, ka, kb, sign):
        ky = ka * (1 - core) + kb * core
        kx = ka * core + kb * (1 - core)
        zz = across(kz, sign)
        yy = (y + sign * ky + side) % side
        xx = (x + sign * kx + side) % side
        return zz, yy * side + xx

    def number(kz, ka, kb):
        return (kz * side + ka) * side + kb

    def remote(src, dst, pair, index, device):
        return pltpu.make_async_remote_copy(
            src_ref=src,
            dst_ref=dst,
            send_sem=pair[0].at[index],
            recv_sem=pair[1].at[index],
            device_id=device,
            device_id_type=MESH,
        )

    started = []

    def send(block, pair, index, device):
        op = remote(block, block, pair, index, device)
        op.start()
        started.append(op)

    def arrive(block, pair, index):
        remote(block, block, pair, index, partner).wait_recv()

    barrier = pltpu.get_barrier_semaphore()
    steps = range(1, side)
    peers = [(kz, 0, 0) for kz in range(1, nz)] + [(0, k // side, k % side) for k in range(1, plane)]
    for peer in peers:
        zz, cc = at(*peer, 1)
        pl.semaphore_signal(barrier, inc=1, device_id=(zz * 2 + core, cc), device_id_type=MESH)
    pl.semaphore_signal(barrier, inc=1, device_id=partner, device_id_type=MESH)

    h = fac_ref[...] * unit
    rbuf[col] = pts_ref[...]
    cbuf[z, core] = pts_ref[...]
    first[col, z, core] = h.astype(jnp.bfloat16)
    pl.semaphore_wait(barrier, len(peers) + 1)

    def gather(ref, pair):
        nchips = nz * plane

        def handle(kz, ka, kb):
            zz, cc = at(kz, ka, kb, -1)
            block = ref.at[cc, zz, core]
            if kz or ka or kb:
                arrive(block, pair, number(kz, ka, kb))
            else:
                for k in range(1, nz):
                    there, _ = at(k, 0, 0, 1)
                    send(block, pair, number(k, 0, 0), (there * 2 + core, col))
            if not kb and not ka:
                for k in range(plane - 1, 0, -1):
                    _, there = at(0, k // side, k % side, 1)
                    send(block, pair, number(kz, k // side, k % side), (row, there))
            send(block, pair, nchips + number(kz, ka, kb), partner)

        def stage(t):
            if t < nz:
                handle(t, 0, 0)
            if 0 <= t - 1 < nz:
                for ka in steps:
                    handle(t - 1, ka, 0)
            if 0 <= t - 2 < nz:
                for ka in range(side):
                    for kb in steps:
                        handle(t - 2, ka, kb)
            if 0 <= t - 3 < nz:
                for ka in range(side):
                    for kb in range(side):
                        zz, cc = at(t - 3, kb, ka, -1)
                        arrive(ref.at[cc, zz, 1 - core], pair, nchips + number(t - 3, ka, kb))
                return across(t - 3, -1)
            return None

        return stage

    zpair, ppair = sems[0], sems[1]
    stage = gather(first, sems[6])
    stage(0)
    for k in range(1, nz):
        there, _ = at(k, 0, 0, 1)
        send(cbuf.at[z, core], zpair, k, (there * 2 + core, col))
    for k in steps:
        _, there = at(0, k, 0, 1)
        send(rbuf.at[col], ppair, number(0, k, 0), (row, there))
    for k in steps:
        _, there = at(0, 0, k, 1)
        send(rbuf.at[col], ppair, number(0, 0, k), (row, there))
    send(cbuf.at[z, core], zpair, nz, partner)
    stage(1)
    for ka in steps:
        _, cc = at(0, ka, 0, -1)
        arrive(rbuf.at[cc], ppair, number(0, ka, 0))
        for k in steps:
            _, there = at(0, 0, k, 1)
            send(rbuf.at[cc], ppair, number(0, ka, k), (row, there))
    for ka in range(side):
        for kb in steps:
            _, cc = at(0, ka, kb, -1)
            arrive(rbuf.at[cc], ppair, number(0, ka, kb))

    def squares(block):
        acc = None
        for k in range(0, width, 128):
            piece = block[:, k : k + 128].astype(jnp.float32)
            acc = piece * piece if acc is None else acc + piece * piece
        return acc

    band, wide = plane * rows, 2 * rows
    tall = min(band, 256)
    row_acc = [None] * (band // tall)
    row_sq = []
    for r in range(band // tall):
        group = tall // rows
        row_sq.append(jnp.sum(squares(rbuf[r * group : (r + 1) * group].reshape(tall, width)), axis=1, keepdims=True))
    mine = row
    tot = jnp.zeros((1, wide), jnp.float32)
    for t in range(2, nz):
        stage(t)
    for kz in range(nz):
        zz = across(kz, -1)
        if kz:
            arrive(cbuf.at[zz, core], zpair, kz)
            send(cbuf.at[zz, core], zpair, nz + kz, partner)
        arrive(cbuf.at[zz, 1 - core], zpair, nz + kz)
        block = cbuf[zz].reshape(wide, width)
        col_sq = jnp.sum(squares(block).T, axis=0, keepdims=True)
        col_acc = jnp.zeros((1, wide), jnp.float32)
        for r in range(band // tall):
            group = tall // rows
            mat = rbuf[r * group : (r + 1) * group].reshape(tall, width)
            gram = lax.dot_general(mat, block, (((1,), (1,)), ((), ())), preferred_element_type=jnp.float32)
            k = jnp.exp((2.0 * gram - row_sq[r] - col_sq) * (0.5 / width))
            kern[zz, r * tall : (r + 1) * tall, :] = k
            row_acc[r] = k if row_acc[r] is None else row_acc[r] + k
            col_acc += jnp.sum(k, axis=0, keepdims=True)
        csum[mine, pl.ds(zz, 1), :] = col_acc
        tot += col_acc
    for r in range(band // tall):
        rsum[col, :, r * tall : (r + 1) * tall] = jnp.sum(row_acc[r].T, axis=0, keepdims=True)
    mydev = row * ncol + col
    tsum[mydev] = tot

    rpair, cpair, tpair = sems[2], sems[3], sems[4]

    def row_copy(k, sign):
        cc = (col + sign * k + ncol) % ncol
        block = rsum.at[col if sign > 0 else cc]
        return remote(block, block, rpair, k, (row, cc))

    def col_copy(k, sign):
        rr = (row + sign * k + nrow) % nrow
        block = csum.at[row if sign > 0 else rr]
        return remote(block, block, cpair, k, (rr, col))

    def tot_copy(k, sign):
        rr, cc = (row + sign * (k // ncol) + nrow) % nrow, (col + sign * (k % ncol) + ncol) % ncol
        block = tsum.at[mydev if sign > 0 else rr * ncol + cc]
        return remote(block, block, tpair, k, (rr, cc))

    def aff_copy(k, sign):
        cc = (col + sign * k + ncol) % ncol
        return remote(asend.at[cc], arecv.at[col if sign > 0 else cc], sems[5], k, (row, cc))

    def each(count, action):
        def body(k, carry):
            action(k)
            return carry

        lax.fori_loop(1, count, body, 0)

    each(ncol, lambda k: row_copy(k, 1).start())
    each(nrow, lambda k: col_copy(k, 1).start())
    each(nrow * ncol, lambda k: tot_copy(k, 1).start())

    for t in range(nz, nz+3):
        stage(t)
    def gram_of(block):
        return lax.dot_general(block, block, (((0,), (0,)), ((), ())), preferred_element_type=jnp.float32)

    def pull(h, hh):
        scale = 0.5 / jnp.sqrt(jnp.sum(hh * hh, keepdims=True) + 1e-06)
        return scale, jnp.dot(h, hh, precision=lax.Precision.HIGHEST, preferred_element_type=jnp.float32)


    each(ncol, lambda k: row_copy(k, -1).wait_recv())
    each(nrow, lambda k: col_copy(k, -1).wait_recv())
    each(nrow * ncol, lambda k: tot_copy(k, -1).wait_recv())
    grand = jnp.sum(jnp.sum(tsum[...], axis=0), axis=1, keepdims=True) / (total * total)
    col_mean = jnp.sum(csum[...], axis=0) / total
    row_mean = jnp.sum(rsum[...], axis=0) / total
    for r in range(band // tall):
        group = tall // rows
        mean_r = jnp.broadcast_to(row_mean[:, r * tall : (r + 1) * tall], (wide, tall)).T
        for zz in range(nz):
            k = kern[zz, r * tall : (r + 1) * tall, :] - mean_r - col_mean[zz : zz + 1, :] + grand
            asend[r * group : (r + 1) * group, zz] = k.astype(jnp.bfloat16).reshape(group, rows, wide)
    arecv[col] = asend[col]
    each(ncol, lambda k: aff_copy(k, 1).start())

    hh = jnp.zeros((rank, rank), jnp.float32)
    for zz in range(nz):
        hh += gram_of(first[:, zz].reshape(plane * wide, rank))
    scale, hhh = pull(h, hh)
    each(ncol, lambda k: aff_copy(k, -1).wait_recv())

    def panel(zz):
        return jnp.concatenate([arecv[c, zz] for c in range(plane)], axis=1)

    ah = jnp.zeros((rows, rank), jnp.float32)
    for zz in range(nz):
        ah += jnp.dot(panel(zz), first[:, zz].reshape(plane * wide, rank), preferred_element_type=jnp.float32)
    h = jnp.maximum(h - scale * (hhh - ah), 0.0)

    later[col, z, core] = h.astype(jnp.bfloat16)
    stage = gather(later, sems[7])
    ah = jnp.zeros((rows, rank), jnp.float32)
    hh = jnp.zeros((rank, rank), jnp.float32)
    for t in range(nz + 3):
        zz = stage(t)
        if zz is not None:
            block = later[:, zz].reshape(plane * wide, rank)
            ah += jnp.dot(panel(zz), block, preferred_element_type=jnp.float32)
            hh += gram_of(block)
    scale, hhh = pull(h, hh)
    out_ref[...] = jnp.maximum(h - scale * (hhh - ah), 0.0) / unit
    for op in started:
        op.wait_send()
    each(ncol, lambda k: row_copy(k, 1).wait_send())
    each(nrow, lambda k: col_copy(k, 1).wait_send())
    each(nrow * ncol, lambda k: tot_copy(k, 1).wait_send())
    each(ncol, lambda k: aff_copy(k, 1).wait_send())


def solution(mesh):
    nrow, ncol = mesh.shape["row"], mesh.shape["col"]
    side = math.isqrt(ncol)
    nz = nrow // 2
    nchips = nz * ncol

    def shards(points, factor):
        rows, width = points.shape
        rank = factor.shape[1]
        wide = 2 * rows
        counts = (2 * nz, ncol, ncol, nrow, nrow * ncol, ncol, 2 * nchips, 2 * nchips)
        return pl.pallas_call(
            functools.partial(kernel, nrow, ncol, side),
            out_shape=jax.ShapeDtypeStruct((rows, rank), jnp.float32),
            in_specs=[pl.BlockSpec(memory_space=pltpu.VMEM)] * 2,
            out_specs=pl.BlockSpec(memory_space=pltpu.VMEM),
            scratch_shapes=[
                pltpu.VMEM((ncol, rows, width), jnp.bfloat16),
                pltpu.VMEM((nz, 2, rows, width), jnp.bfloat16),
                pltpu.VMEM((ncol, nz, 2, rows, rank), jnp.bfloat16),
                pltpu.VMEM((ncol, nz, 2, rows, rank), jnp.bfloat16),
                pltpu.VMEM((nz, ncol * rows, wide), jnp.float32),
                pltpu.VMEM((ncol, nz, rows, wide), jnp.bfloat16),
                pltpu.VMEM((ncol, nz, rows, wide), jnp.bfloat16),
                pltpu.VMEM((ncol, 1, ncol * rows), jnp.float32),
                pltpu.VMEM((nrow, nz, wide), jnp.float32),
                pltpu.VMEM((nrow * ncol, 1, wide), jnp.float32),
                [(pltpu.SemaphoreType.DMA((n,)), pltpu.SemaphoreType.DMA((n,))) for n in counts],
            ],
            compiler_params=pltpu.CompilerParams(
                collective_id=0, has_side_effects=True, vmem_limit_bytes=67043328
            ),
        )(points, factor)

    spec = P(("row", "col"), None)
    return jax.shard_map(shards, mesh=mesh, in_specs=(spec, spec), out_specs=spec, check_vma=False)
```

```python
import functools
import math

import jax
import jax.numpy as jnp
from jax import lax
from jax.experimental import pallas as pl
from jax.experimental.pallas import tpu as pltpu
from jax.sharding import PartitionSpec as P

MESH = pl.DeviceIdType.MESH


def kernel(nrow, ncol, side, pts_ref, fac_ref, out_ref, rbuf, cbuf, first, later, kern, asend, arecv, rsum, csum, tsum, sems):
    nz, plane = nrow // 2, ncol
    rows, width = pts_ref.shape
    rank = fac_ref.shape[1]
    total = rows * nrow * ncol
    unit = 2.0 / math.sqrt(total * rank)
    row, col = lax.axis_index("row"), lax.axis_index("col")
    z, core = row // 2, row % 2
    y, x = col // side, col % side
    partner = (z * 2 + 1 - core, col)

    def across(kz, sign):
        if nz & (nz - 1):
            return (z + sign * kz + nz) % nz
        zz, bit = z, 1
        while bit < nz:
            if kz & bit:
                zz = zz + bit - 2 * bit * ((z // bit) % 2)
            bit *= 2
        return zz

    def at(kz, ka, kb, sign):
        ky = ka * (1 - core) + kb * core
        kx = ka * core + kb * (1 - core)
        zz = across(kz, sign)
        yy = (y + sign * ky + side) % side
        xx = (x + sign * kx + side) % side
        return zz, yy * side + xx

    def number(kz, ka, kb):
        return (kz * side + ka) * side + kb

    def remote(src, dst, pair, index, device):
        return pltpu.make_async_remote_copy(
            src_ref=src,
            dst_ref=dst,
            send_sem=pair[0].at[index],
            recv_sem=pair[1].at[index],
            device_id=device,
            device_id_type=MESH,
        )

    started = []

    def send(block, pair, index, device):
        op = remote(block, block, pair, index, device)
        op.start()
        started.append(op)

    def arrive(block, pair, index):
        remote(block, block, pair, index, partner).wait_recv()

    barrier = pltpu.get_barrier_semaphore()
    steps = range(1, side)
    peers = [(kz, 0, 0) for kz in range(1, nz)] + [(0, k // side, k % side) for k in range(1, plane)]
    for peer in peers:
        zz, cc = at(*peer, 1)
        pl.semaphore_signal(barrier, inc=1, device_id=(zz * 2 + core, cc), device_id_type=MESH)
    pl.semaphore_signal(barrier, inc=1, device_id=partner, device_id_type=MESH)

    h = fac_ref[...] * unit
    rbuf[col] = pts_ref[...]
    cbuf[z, core] = pts_ref[...]
    first[col, z, core] = h.astype(jnp.bfloat16)
    pl.semaphore_wait(barrier, len(peers) + 1)

    def gather(ref, pair):
        nchips = nz * plane

        def handle(kz, ka, kb):
            zz, cc = at(kz, ka, kb, -1)
            block = ref.at[cc, zz, core]
            if kz or ka or kb:
                arrive(block, pair, number(kz, ka, kb))
            else:
                for k in range(1, nz):
                    there, _ = at(k, 0, 0, 1)
                    send(block, pair, number(k, 0, 0), (there * 2 + core, col))
            send(block, pair, nchips + number(kz, ka, kb), partner)
            if not kb and not ka:
                for k in range(plane - 1, 0, -1):
                    _, there = at(0, k // side, k % side, 1)
                    send(block, pair, number(kz, k // side, k % side), (row, there))

        def stage(t):
            if t < nz:
                handle(t, 0, 0)
            if 0 <= t - 1 < nz:
                for ka in steps:
                    handle(t - 1, ka, 0)
            if 0 <= t - 2 < nz:
                for ka in range(side):
                    for kb in steps:
                        handle(t - 2, ka, kb)
            if 0 <= t - 3 < nz:
                for ka in range(side):
                    for kb in range(side):
                        zz, cc = at(t - 3, kb, ka, -1)
                        arrive(ref.at[cc, zz, 1 - core], pair, nchips + number(t - 3, ka, kb))
                return across(t - 3, -1)
            return None

        return stage

    zpair, ppair = sems[0], sems[1]
    stage = gather(first, sems[6])
    stage(0)
    for k in range(1, nz):
        there, _ = at(k, 0, 0, 1)
        send(cbuf.at[z, core], zpair, k, (there * 2 + core, col))
    for k in steps:
        _, there = at(0, k, 0, 1)
        send(rbuf.at[col], ppair, number(0, k, 0), (row, there))
    for k in steps:
        _, there = at(0, 0, k, 1)
        send(rbuf.at[col], ppair, number(0, 0, k), (row, there))
    send(cbuf.at[z, core], zpair, nz, partner)
    stage(1)
    for ka in steps:
        _, cc = at(0, ka, 0, -1)
        arrive(rbuf.at[cc], ppair, number(0, ka, 0))
        for k in steps:
            _, there = at(0, 0, k, 1)
            send(rbuf.at[cc], ppair, number(0, ka, k), (row, there))
    for ka in range(side):
        for kb in steps:
            _, cc = at(0, ka, kb, -1)
            arrive(rbuf.at[cc], ppair, number(0, ka, kb))

    def squares(block):
        acc = None
        for k in range(0, width, 128):
            piece = block[:, k : k + 128].astype(jnp.float32)
            acc = piece * piece if acc is None else acc + piece * piece
        return acc

    band, wide = plane * rows, 2 * rows
    tall = min(band, 256)
    row_acc = [None] * (band // tall)
    row_sq = []
    for r in range(band // tall):
        group = tall // rows
        row_sq.append(jnp.sum(squares(rbuf[r * group : (r + 1) * group].reshape(tall, width)), axis=1, keepdims=True))
    mine = row
    tot = jnp.zeros((1, wide), jnp.float32)
    for t in range(2, nz):
        stage(t)
    for kz in range(nz):
        zz = across(kz, -1)
        if kz:
            arrive(cbuf.at[zz, core], zpair, kz)
            send(cbuf.at[zz, core], zpair, nz + kz, partner)
        arrive(cbuf.at[zz, 1 - core], zpair, nz + kz)
        block = cbuf[zz].reshape(wide, width)
        col_sq = jnp.sum(squares(block).T, axis=0, keepdims=True)
        col_acc = jnp.zeros((1, wide), jnp.float32)
        for r in range(band // tall):
            group = tall // rows
            mat = rbuf[r * group : (r + 1) * group].reshape(tall, width)
            gram = lax.dot_general(mat, block, (((1,), (1,)), ((), ())), preferred_element_type=jnp.float32)
            k = jnp.exp((2.0 * gram - row_sq[r] - col_sq) * (0.5 / width))
            kern[zz, r * tall : (r + 1) * tall, :] = k
            row_acc[r] = k if row_acc[r] is None else row_acc[r] + k
            col_acc += jnp.sum(k, axis=0, keepdims=True)
        csum[mine, pl.ds(zz, 1), :] = col_acc
        tot += col_acc
    for r in range(band // tall):
        rsum[col, :, r * tall : (r + 1) * tall] = jnp.sum(row_acc[r].T, axis=0, keepdims=True)
    mydev = row * ncol + col
    tsum[mydev] = tot

    rpair, cpair, tpair = sems[2], sems[3], sems[4]

    def row_copy(k, sign):
        cc = (col + sign * k + ncol) % ncol
        block = rsum.at[col if sign > 0 else cc]
        return remote(block, block, rpair, k, (row, cc))

    def col_copy(k, sign):
        rr = (row + sign * k + nrow) % nrow
        block = csum.at[row if sign > 0 else rr]
        return remote(block, block, cpair, k, (rr, col))

    def tot_copy(k, sign):
        rr, cc = (row + sign * (k // ncol) + nrow) % nrow, (col + sign * (k % ncol) + ncol) % ncol
        block = tsum.at[mydev if sign > 0 else rr * ncol + cc]
        return remote(block, block, tpair, k, (rr, cc))

    def aff_copy(k, sign):
        cc = (col + sign * k + ncol) % ncol
        return remote(asend.at[cc], arecv.at[col if sign > 0 else cc], sems[5], k, (row, cc))

    def each(count, action):
        def body(k, carry):
            action(k)
            return carry

        lax.fori_loop(1, count, body, 0, unroll=count <= 32)

    each(nrow * ncol, lambda k: tot_copy(k, 1).start())
    each(ncol, lambda k: row_copy(k, 1).start())
    each(nrow, lambda k: col_copy(k, 1).start())

    for t in range(nz, nz+3):
        stage(t)
    def gram_of(block):
        return lax.dot_general(block, block, (((0,), (0,)), ((), ())), preferred_element_type=jnp.float32)

    def pull(h, hh):
        scale = 0.5 / jnp.sqrt(jnp.sum(hh * hh, keepdims=True) + 1e-06)
        return scale, jnp.dot(h, hh, precision=lax.Precision.HIGHEST, preferred_element_type=jnp.float32)


    each(ncol, lambda k: row_copy(k, -1).wait_recv())
    each(nrow, lambda k: col_copy(k, -1).wait_recv())
    each(nrow * ncol, lambda k: tot_copy(k, -1).wait_recv())
    grand = jnp.sum(jnp.sum(tsum[...], axis=0), axis=1, keepdims=True) / (total * total)
    col_mean = jnp.sum(csum[...], axis=0) / total
    row_mean = jnp.sum(rsum[...], axis=0) / total
    for r in range(band // tall):
        group = tall // rows
        mean_r = jnp.broadcast_to(row_mean[:, r * tall : (r + 1) * tall], (wide, tall)).T
        for zz in range(nz):
            k = kern[zz, r * tall : (r + 1) * tall, :] - mean_r - col_mean[zz : zz + 1, :] + grand
            asend[r * group : (r + 1) * group, zz] = k.astype(jnp.bfloat16).reshape(group, rows, wide)
    arecv[col] = asend[col]
    each(ncol, lambda k: aff_copy(k, 1).start())

    hh = jnp.zeros((rank, rank), jnp.float32)
    for zz in range(nz):
        hh += gram_of(first[:, zz].reshape(plane * wide, rank))
    scale, hhh = pull(h, hh)
    each(ncol, lambda k: aff_copy(k, -1).wait_recv())

    def panel(zz):
        return jnp.concatenate([arecv[c, zz] for c in range(plane)], axis=1)

    ah = jnp.zeros((rows, rank), jnp.float32)
    for zz in range(nz):
        ah += jnp.dot(panel(zz), first[:, zz].reshape(plane * wide, rank), preferred_element_type=jnp.float32)
    h = jnp.maximum(h - scale * (hhh - ah), 0.0)

    later[col, z, core] = h.astype(jnp.bfloat16)
    stage = gather(later, sems[7])
    ah = jnp.zeros((rows, rank), jnp.float32)
    hh = jnp.zeros((rank, rank), jnp.float32)
    for t in range(nz + 3):
        zz = stage(t)
        if zz is not None:
            block = later[:, zz].reshape(plane * wide, rank)
            ah += jnp.dot(panel(zz), block, preferred_element_type=jnp.float32)
            hh += gram_of(block)
    scale, hhh = pull(h, hh)
    out_ref[...] = jnp.maximum(h - scale * (hhh - ah), 0.0) / unit
    for op in started:
        op.wait_send()
    each(ncol, lambda k: row_copy(k, 1).wait_send())
    each(nrow, lambda k: col_copy(k, 1).wait_send())
    each(nrow * ncol, lambda k: tot_copy(k, 1).wait_send())
    each(ncol, lambda k: aff_copy(k, 1).wait_send())


def solution(mesh):
    nrow, ncol = mesh.shape["row"], mesh.shape["col"]
    side = math.isqrt(ncol)
    nz = nrow // 2
    nchips = nz * ncol

    def shards(points, factor):
        rows, width = points.shape
        rank = factor.shape[1]
        wide = 2 * rows
        counts = (2 * nz, ncol, ncol, nrow, nrow * ncol, ncol, 2 * nchips, 2 * nchips)
        return pl.pallas_call(
            functools.partial(kernel, nrow, ncol, side),
            out_shape=jax.ShapeDtypeStruct((rows, rank), jnp.float32),
            in_specs=[pl.BlockSpec(memory_space=pltpu.VMEM)] * 2,
            out_specs=pl.BlockSpec(memory_space=pltpu.VMEM),
            scratch_shapes=[
                pltpu.VMEM((ncol, rows, width), jnp.bfloat16),
                pltpu.VMEM((nz, 2, rows, width), jnp.bfloat16),
                pltpu.VMEM((ncol, nz, 2, rows, rank), jnp.bfloat16),
                pltpu.VMEM((ncol, nz, 2, rows, rank), jnp.bfloat16),
                pltpu.VMEM((nz, ncol * rows, wide), jnp.float32),
                pltpu.VMEM((ncol, nz, rows, wide), jnp.bfloat16),
                pltpu.VMEM((ncol, nz, rows, wide), jnp.bfloat16),
                pltpu.VMEM((ncol, 1, ncol * rows), jnp.float32),
                pltpu.VMEM((nrow, nz, wide), jnp.float32),
                pltpu.VMEM((nrow * ncol, 1, wide), jnp.float32),
                [(pltpu.SemaphoreType.DMA((n,)), pltpu.SemaphoreType.DMA((n,))) for n in counts],
            ],
            compiler_params=pltpu.CompilerParams(
                collective_id=0, has_side_effects=True, vmem_limit_bytes=67043328
            ),
        )(points, factor)

    spec = P(("row", "col"), None)
    return jax.shard_map(shards, mesh=mesh, in_specs=(spec, spec), out_specs=spec, check_vma=False)
```
